256 devices in a mesh: row: 16 (over x, y), col: 16 (over z, core).
Axes of the slice: x: 4, y: 4, z: 8, core: 2. Of those that a mesh axis runs over, the one named last changes fastest.
Arguments:
- features: bfloat16 [65536, 256], P(('col', 'row')), may hold values from -6 to 6
- cotangent: bfloat16 [65536, 256], P(('row', 'col')), may hold values from -1.5 to 1.5
- degrees: int32 [65536], P(('row', 'col')), may hold values from 8 to 40
- weight: bfloat16 [256, 256], replicated, may hold values from -0.375 to 0.375
- tile_rows: int32 [16, 16, 256], P('row', 'col'), may hold values from 0 to 31
- tile_cols: int32 [16, 16, 256], P('row', 'col'), may hold values from 0 to 31
- tile_bits: int32 [16, 16, 256, 16, 128], P('row', 'col'), may hold values from 0 to 255, as said below
- tile_count: int32 [16, 16], P('row', 'col'), may hold values from 16 to 256, as said below
Outputs:
- output: bfloat16 [65536, 256], P(('row', 'col'))
- weight_grad: float32 [256, 256], replicated
- input_grad: bfloat16 [65536, 256], P(('col', 'row'))
The draws below stay inside these ranges and needn't reach their ends.
Inputs may be any that keep to these rules, and one draw needn't show every extreme that they name: `tile_bits`: each word holds 8 entries of 0 or 1 in its low bits; tiles at the same position may repeat and then add. `tile_count`: some device has all 256 slots live and some device 256 // 16.
All inputs are finite; a program needn't handle non-finite values.
Results may differ from the reference program's by a relative error of at most 0.024.
Values may be sent and summed in bfloat16 or wider, within the bound.
No kernel may reach another device: no remote copies, remote signals or barrier semaphores. Data moves between devices by JAX's collectives and lax.ppermute only.
A program may use at most 64 MiB of HBM per device.

```python
import math
import jax
import jax.numpy as jnp
from jax import lax

F = 256
TILE = 128
NP = 256
TILES_DEV = 256
NODES = 65536
TROWS = 32
TCOLS = 32
N_ROW = 16
N_COL = 16


def draw_tile_bits(key, part):
    shape = (N_ROW, N_COL, TILES_DEV, TILE // 8, TILE)
    packed = jnp.zeros(shape, jnp.int32)
    for bit_number in range(8):
        flags = (jax.random.randint(jax.random.fold_in(key, 101 + bit_number), shape, 0, TILE) == 0).astype(jnp.int32)
        packed = packed + flags * 2 ** bit_number
    return packed


def draw_tile_count(key, part):
    devices_all = N_ROW * N_COL
    counted = jax.random.randint(jax.random.fold_in(key, 7), (devices_all,), TILES_DEV // 16, TILES_DEV + 1)
    shuffled = jax.random.permutation(jax.random.fold_in(key, 8), devices_all)
    counted = counted.at[shuffled[0]].set(TILES_DEV)
    counted = counted.at[shuffled[1]].set(TILES_DEV // 16)
    return counted.astype(jnp.int32).reshape(N_ROW, N_COL)


def place_ends(drawn, stream_key, low, top_value):
    spot = [jax.random.randint(jax.random.fold_in(stream_key, axis), (), 0, length) for axis, length in enumerate(drawn.shape)]
    main_axis = drawn.shape.index(max(drawn.shape))
    next_to = spot[:main_axis] + [(spot[main_axis] + 1) % drawn.shape[main_axis]] + spot[main_axis + 1:]
    return drawn.at[tuple(spot)].set(low).at[tuple(next_to)].set(top_value)


def levels(key, dims, cuts, low, top_value):
    level = 1.0
    for dim, parts in cuts:
        draws = jax.random.uniform(jax.random.fold_in(jax.random.fold_in(key, 6), dim), (parts,), jnp.float32, low / len(cuts), top_value / len(cuts))
        level = level * jnp.repeat(jnp.exp(draws), dims[dim] // parts).reshape((-1,) + (1,) * (len(dims) - 1 - dim))
    return level


def centred(rng, dims, spread, limit, split=(), held_as=jnp.bfloat16):
    level = levels(rng, dims, split, -0.22, 0.18) if split else 1.0
    array = jax.random.normal(rng, dims, jnp.float32) * spread * level
    return jnp.minimum(jnp.maximum(array, -limit), limit).astype(held_as)


def setup_inputs(seed: int = 0) -> dict:
    splits = jax.random.split(jax.random.key(seed), 9)
    features = centred(splits[0], (NODES, F), 1.0, 6.0, ((0, 256),))
    cotangent = centred(splits[1], (NODES, F), 0.25, 1.5, ((0, 256),))
    degrees = place_ends(jax.random.randint(splits[2], (NODES,), 8, 41), jax.random.fold_in(splits[2], 1), 8, 40).astype(jnp.int32)
    weight = centred(splits[3], (F, F), F ** -0.5, 0.375)
    tile_rows = place_ends(jax.random.randint(splits[4], (N_ROW, N_COL, TILES_DEV), 0, TROWS), jax.random.fold_in(splits[4], 1), 0, TROWS - 1).astype(jnp.int32)
    tile_cols = place_ends(jax.random.randint(splits[5], (N_ROW, N_COL, TILES_DEV), 0, TCOLS), jax.random.fold_in(splits[5], 1), 0, TCOLS - 1).astype(jnp.int32)
    tile_bits = draw_tile_bits(jax.random.fold_in(splits[8], 71), 0)
    tile_count = draw_tile_count(jax.random.fold_in(splits[8], 71), 0)
    return dict(features=features, cotangent=cotangent, degrees=degrees, weight=weight, tile_rows=tile_rows, tile_cols=tile_cols, tile_bits=tile_bits, tile_count=tile_count)


def unpack(packed):
    shifts = jnp.arange(8, dtype=jnp.int32)
    flags = jnp.right_shift(packed[:, :, None, :], shifts[None, None, :, None]) & 1
    return flags.reshape(packed.shape[0], packed.shape[1] * 8, packed.shape[2])


def sweep_tiles(packed, row_ids, col_ids, live_count, source, out_tiles, forward):
    block_size = math.gcd(TILES_DEV, 32)

    def one_block(totals, position):
        offset = position * block_size
        block_bits = lax.dynamic_slice_in_dim(packed, offset, block_size, 0)
        block_rows = lax.dynamic_slice_in_dim(row_ids, offset, block_size, 0)
        block_cols = lax.dynamic_slice_in_dim(col_ids, offset, block_size, 0)
        live_mask = (offset + jnp.arange(block_size, dtype=jnp.int32)) < live_count
        pattern = (unpack(block_bits) * live_mask.astype(jnp.int32)[:, None, None]).astype(jnp.float32)
        if forward:
            product = jnp.einsum("bji,bjf->bif", pattern, source[block_cols])
            return totals.at[block_rows].add(product), None
        product = jnp.einsum("bji,bif->bjf", pattern, source[block_rows])
        return totals.at[block_cols].add(product), None

    initial = jnp.zeros((out_tiles, TILE, F), jnp.float32)
    totals, _ = lax.scan(one_block, initial, jnp.arange(TILES_DEV // block_size, dtype=jnp.int32))
    return totals


def rounded(values):
    return lax.optimization_barrier(values.astype(jnp.bfloat16)).astype(jnp.float32)


def reference(features, cotangent, degrees, weight, tile_rows, tile_cols, tile_bits, tile_count):
    rows_block = NP * N_COL
    cols_block = NP * N_ROW
    degree_values = degrees.astype(jnp.float32)
    feature_tiles = features.astype(jnp.float32).reshape(N_COL, cols_block // TILE, TILE, F)
    scaled = (cotangent.astype(jnp.float32) / degree_values[:, None]).astype(jnp.bfloat16)
    gradient_tiles = scaled.astype(jnp.float32).reshape(N_ROW, rows_block // TILE, TILE, F)

    def forward_row(row_block):
        def add_column(running, col_block):
            partial_value = sweep_tiles(tile_bits[row_block, col_block], tile_rows[row_block, col_block],
                                  tile_cols[row_block, col_block], tile_count[row_block, col_block],
                                  feature_tiles[col_block], rows_block // TILE, True)
            return running + rounded(partial_value), None
        start_sum = jnp.zeros((rows_block // TILE, TILE, F), jnp.float32)
        running, _ = lax.scan(add_column, start_sum, jnp.arange(N_COL, dtype=jnp.int32))
        return running.reshape(rows_block, F)

    def backward_column(col_block):
        def add_row(running, row_block):
            partial_value = sweep_tiles(tile_bits[row_block, col_block], tile_rows[row_block, col_block],
                                  tile_cols[row_block, col_block], tile_count[row_block, col_block],
                                  gradient_tiles[row_block], cols_block // TILE, False)
            return running + rounded(partial_value), None
        start_sum = jnp.zeros((cols_block // TILE, TILE, F), jnp.float32)
        running, _ = lax.scan(add_row, start_sum, jnp.arange(N_ROW, dtype=jnp.int32))
        return running.reshape(cols_block, F)

    summed = lax.map(forward_row, jnp.arange(N_ROW, dtype=jnp.int32)).reshape(NODES, F)
    aggregated = (summed / degree_values[:, None]).astype(jnp.bfloat16)
    output = jnp.dot(aggregated, weight, preferred_element_type=jnp.float32).astype(jnp.bfloat16)
    weight_grad = jnp.dot(aggregated.T, cotangent, preferred_element_type=jnp.float32)
    propagated = lax.map(backward_column, jnp.arange(N_COL, dtype=jnp.int32)).reshape(NODES, F)
    input_grad = jnp.dot(propagated.astype(jnp.bfloat16), weight.T, preferred_element_type=jnp.float32).astype(jnp.bfloat16)
    return output, weight_grad, input_grad
```

```python
import functools

import jax
import jax.numpy as jnp
from jax import lax
from jax.experimental import pallas as pl
from jax.experimental.pallas import tpu as pltpu
from jax.sharding import PartitionSpec as P

BLOCK = 64
VMEM = 56 << 20


def unpack(words):
    depth, tile = words.shape
    bit = jnp.left_shift(1, lax.broadcasted_iota(jnp.int32, (1, 8, tile), 1))
    wide = jnp.broadcast_to(words[:, None, :], (depth, 8, tile))
    return jnp.where((wide & bit) != 0, 1.0, 0.0).reshape(depth * 8, tile)


def add_tiles(count_ref, to_ref, from_ref, bits_ref, source_ref, total, contract):
    step = pl.program_id(0)
    block = bits_ref.shape[0]

    @pl.when(step == 0)
    def _():
        total[...] = jnp.zeros_like(total)

    @pl.when(step * block < count_ref[0])
    def _():
        for k in range(block):
            slot = step * block + k
            product = lax.dot_general(
                unpack(bits_ref[k]).astype(jnp.bfloat16),
                source_ref[from_ref[slot]],
                (((contract,), (0,)), ((), ())),
                preferred_element_type=jnp.float32,
            )
            total[to_ref[slot]] += product


def forward_body(count_ref, to_ref, from_ref, bits_ref, source_ref, own_ref, other_ref, total):
    add_tiles(count_ref, to_ref, from_ref, bits_ref, source_ref, total, 0)

    @pl.when(pl.program_id(0) == pl.num_programs(0) - 1)
    def _():
        blocks = own_ref.shape[0]
        own_ref[...] = total[:blocks].astype(own_ref.dtype)
        other_ref[...] = total[blocks : 2 * blocks].astype(other_ref.dtype)


def forward_sweep(count, to_ids, from_ids, bits, source):
    slots, depth, tile = bits.shape
    blocks, _, width = source.shape
    out = jax.ShapeDtypeStruct((blocks // 2, tile, width), jnp.bfloat16)
    out_spec = pl.BlockSpec(out.shape, lambda i, *_: (0, 0, 0))
    return pl.pallas_call(
        forward_body,
        out_shape=(out, out),
        grid_spec=pltpu.PrefetchScalarGridSpec(
            num_scalar_prefetch=3,
            grid=(slots // BLOCK,),
            in_specs=[
                pl.BlockSpec((BLOCK, depth, tile), lambda i, *_: (i, 0, 0)),
                pl.BlockSpec(source.shape, lambda i, *_: (0, 0, 0)),
            ],
            out_specs=(out_spec, out_spec),
            scratch_shapes=[pltpu.VMEM((blocks + 1, tile, width), jnp.float32)],
        ),
        compiler_params=pltpu.CompilerParams(vmem_limit_bytes=VMEM),
        cost_estimate=pl.CostEstimate(
            flops=slots * tile * tile * width * 2,
            bytes_accessed=bits.size * 4 + source.size * 4,
            transcendentals=0,
        ),
        name="forward_sweep",
    )(count, to_ids, from_ids, bits, source)


def backward_body(count_ref, to_ref, from_ref, bits_ref, source_ref, out_ref, total):
    add_tiles(count_ref, to_ref, from_ref, bits_ref, source_ref, total, 1)

    @pl.when(pl.program_id(0) == pl.num_programs(0) - 1)
    def _():
        out_ref[...] = total[: out_ref.shape[0]].astype(out_ref.dtype)


def backward_sweep(count, to_ids, from_ids, bits, source):
    slots, depth, tile = bits.shape
    blocks, _, width = source.shape
    out = jax.ShapeDtypeStruct((blocks, tile, width), jnp.bfloat16)
    return pl.pallas_call(
        backward_body,
        out_shape=out,
        grid_spec=pltpu.PrefetchScalarGridSpec(
            num_scalar_prefetch=3,
            grid=(slots // BLOCK,),
            in_specs=[
                pl.BlockSpec((BLOCK, depth, tile), lambda i, *_: (i, 0, 0)),
                pl.BlockSpec(source.shape, lambda i, *_: (0, 0, 0)),
            ],
            out_specs=pl.BlockSpec(out.shape, lambda i, *_: (0, 0, 0)),
            scratch_shapes=[pltpu.VMEM((blocks + 1, tile, width), jnp.float32)],
        ),
        compiler_params=pltpu.CompilerParams(vmem_limit_bytes=VMEM),
        cost_estimate=pl.CostEstimate(
            flops=slots * tile * tile * width * 2,
            bytes_accessed=bits.size * 4 + source.size * 4,
            transcendentals=0,
        ),
        name="backward_sweep",
    )(count, to_ids, from_ids, bits, source)


def pack_body(partial_ref, features_ref, out_ref):
    owners, rows, width = out_ref.shape
    nodes = partial_ref.shape[1]
    term = jnp.zeros((width, width), jnp.float32)
    for owner in range(owners):
        part = partial_ref[owner]
        out_ref[owner, :nodes] = part
        term += lax.dot_general(
            features_ref[owner], part, (((0,), (0,)), ((), ())), preferred_element_type=jnp.float32
        )
    for owner in range(owners):
        share = term[owner * (rows - nodes) : (owner + 1) * (rows - nodes)]
        out_ref[owner, nodes:] = share.astype(out_ref.dtype)


def pack(partial, features):
    owners, nodes, width = features.shape
    out = jax.ShapeDtypeStruct((owners, nodes + width // owners, width), jnp.bfloat16)
    whole = pl.BlockSpec(memory_space=pltpu.VMEM)
    return pl.pallas_call(
        pack_body,
        out_shape=out,
        in_specs=[whole, whole],
        out_specs=whole,
        cost_estimate=pl.CostEstimate(
            flops=features.size * width * 2, bytes_accessed=features.size * 6, transcendentals=0
        ),
        name="pack",
    )(partial, features)


def spread(block, axis):
    copies = lax.axis_size(axis)
    return lax.all_to_all(jnp.broadcast_to(block[None], (copies, *block.shape)), axis, 0, 0)


def swap_cores(block):
    return lax.ppermute(block, "col", [(i, i ^ 1) for i in range(lax.axis_size("col"))])


def swap_chips(block):
    return lax.ppermute(block, "col", [(i, i ^ 2) for i in range(lax.axis_size("col"))])


def from_below(block, distance):
    n_col = lax.axis_size("col")
    return lax.ppermute(block, "col", [(i, (i + 2 * distance) % n_col) for i in range(n_col)])


def per_device(features, cotangent, degrees, weight, tile_rows, tile_cols, tile_bits, tile_count):
    row_ids, col_ids, count = tile_rows[0, 0], tile_cols[0, 0], tile_count[0]
    tile = tile_bits.shape[-1]
    nodes, width = features.shape
    n_row, n_col = lax.axis_size("row"), lax.axis_size("col")
    n_z = n_col // 2
    place = lax.axis_index("col")
    core, z = place % 2, place // 2
    core_id = core.astype(jnp.int32)[None]
    degree = degrees[:, None].astype(jnp.float32)

    bits = tile_bits[0, 0]
    blocks = n_row * nodes // tile

    copies = jnp.broadcast_to(features[None], (n_row, nodes, width))
    source = lax.all_to_all(copies, "row", 0, 0)
    scaled = (cotangent.astype(jnp.float32) / degree).astype(jnp.bfloat16)
    own = jnp.stack([scaled] + [from_below(scaled, d) for d in range(1, n_z)])
    gradient = jnp.concatenate([own, swap_cores(own)])

    live = jnp.arange(row_ids.shape[0], dtype=jnp.int32) < count
    owner, half = row_ids // 2, row_ids % 2
    side = (owner % 2 != core) * n_z
    row_sources = (side + jnp.remainder(z - owner // 2, n_z)) * 2 + half
    apart = (owner // 2 + z) % 2 * (n_z // 2)
    away = jnp.remainder(owner // 4 - z // 2, n_z // 2)
    row_targets = (side + apart + away) * 2 + half
    row_targets = jnp.where(live, row_targets, blocks)
    col_targets = jnp.where(live, col_ids, blocks)

    partial = backward_sweep(
        count, col_targets, row_sources, bits, gradient.reshape(-1, tile, width)
    )
    partial = pack(partial.reshape(n_row, nodes, width), source)
    shares = lax.all_to_all(partial, "row", 0, 0)

    kept, sent = forward_sweep(count, row_targets, col_ids, bits, source.reshape(-1, tile, width))
    chip = kept.astype(jnp.float32) + swap_cores(sent).astype(jnp.float32)
    chip = chip.reshape(2, n_z // 2, nodes, width)
    got = swap_chips(chip[1].astype(jnp.bfloat16))
    pair = (chip[0] + got.astype(jnp.float32)).astype(jnp.bfloat16)
    pieces = [pair[0]] + [from_below(pair[k], 2 * k) for k in range(1, n_z // 2)]
    summed = sum(p.astype(jnp.float32) for p in pieces)

    shares = shares.astype(jnp.float32).sum(0)
    term = spread(shares[nodes:], "col").sum(0)
    weight_grad = spread(term, "row").reshape(width, width)
    propagated = shares[:nodes].astype(jnp.bfloat16)
    input_grad = jnp.dot(propagated, weight.T, preferred_element_type=jnp.float32).astype(
        jnp.bfloat16
    )
    aggregated = (summed / degree).astype(jnp.bfloat16)
    output = jnp.dot(aggregated, weight, preferred_element_type=jnp.float32).astype(jnp.bfloat16)
    return output, weight_grad, input_grad


def solution(mesh):
    placed = (
        P(("col", "row"), None),
        P(("row", "col"), None),
        P(("row", "col")),
        P(),
        P("row", "col", None),
        P("row", "col", None),
        P("row", "col", None, None, None),
        P("row", "col"),
    )
    return jax.shard_map(
        per_device,
        mesh=mesh,
        in_specs=placed,
        out_specs=(P(("row", "col"), None), P(), P(("col", "row"), None)),
        check_vma=False,
    )
```

```python
import functools

import jax
import jax.numpy as jnp
from jax import lax
from jax.experimental import pallas as pl
from jax.experimental.pallas import tpu as pltpu
from jax.sharding import PartitionSpec as P

BLOCK = 64
VMEM = 24 << 20


def unpack(words):
    depth, tile = words.shape
    bit = jnp.left_shift(1, lax.broadcasted_iota(jnp.int32, (1, 8, tile), 1))
    wide = jnp.broadcast_to(words[:, None, :], (depth, 8, tile))
    return jnp.where((wide & bit) != 0, 1.0, 0.0).reshape(depth * 8, tile)


def add_tiles(count_ref, to_ref, from_ref, bits_ref, source_ref, total, contract):
    step = pl.program_id(0)
    block = bits_ref.shape[0]

    @pl.when(step == 0)
    def _():
        total[...] = jnp.zeros_like(total)

    @pl.when(step * block < count_ref[0])
    def _():
        for k in range(block):
            slot = step * block + k
            product = lax.dot_general(
                unpack(bits_ref[k]).astype(jnp.bfloat16),
                source_ref[from_ref[slot]],
                (((contract,), (0,)), ((), ())),
                preferred_element_type=jnp.float32,
            )
            total[to_ref[slot]] += product


def forward_body(count_ref, to_ref, from_ref, bits_ref, source_ref, own_ref, other_ref, total):
    add_tiles(count_ref, to_ref, from_ref, bits_ref, source_ref, total, 0)

    @pl.when(pl.program_id(0) == pl.num_programs(0) - 1)
    def _():
        blocks = own_ref.shape[0]
        own_ref[...] = total[:blocks].astype(own_ref.dtype)
        other_ref[...] = total[blocks : 2 * blocks].astype(other_ref.dtype)


def forward_sweep(count, to_ids, from_ids, bits, source):
    slots, depth, tile = bits.shape
    blocks, _, width = source.shape
    out = jax.ShapeDtypeStruct((blocks // 2, tile, width), jnp.bfloat16)
    out_spec = pl.BlockSpec(out.shape, lambda i, *_: (0, 0, 0))
    return pl.pallas_call(
        forward_body,
        out_shape=(out, out),
        grid_spec=pltpu.PrefetchScalarGridSpec(
            num_scalar_prefetch=3,
            grid=(slots // BLOCK,),
            in_specs=[
                pl.BlockSpec((BLOCK, depth, tile), lambda i, *_: (i, 0, 0)),
                pl.BlockSpec(source.shape, lambda i, *_: (0, 0, 0)),
            ],
            out_specs=(out_spec, out_spec),
            scratch_shapes=[pltpu.VMEM((blocks + 1, tile, width), jnp.float32)],
        ),
        compiler_params=pltpu.CompilerParams(vmem_limit_bytes=VMEM),
        cost_estimate=pl.CostEstimate(
            flops=slots * tile * tile * width * 2,
            bytes_accessed=bits.size * 4 + source.size * 4,
            transcendentals=0,
        ),
        name="forward_sweep",
    )(count, to_ids, from_ids, bits, source)


def backward_body(count_ref, to_ref, from_ref, bits_ref, source_ref, out_ref, total):
    add_tiles(count_ref, to_ref, from_ref, bits_ref, source_ref, total, 1)

    @pl.when(pl.program_id(0) == pl.num_programs(0) - 1)
    def _():
        out_ref[...] = total[: out_ref.shape[0]].astype(out_ref.dtype)


def backward_sweep(count, to_ids, from_ids, bits, source):
    slots, depth, tile = bits.shape
    blocks, _, width = source.shape
    out = jax.ShapeDtypeStruct((blocks, tile, width), jnp.bfloat16)
    return pl.pallas_call(
        backward_body,
        out_shape=out,
        grid_spec=pltpu.PrefetchScalarGridSpec(
            num_scalar_prefetch=3,
            grid=(slots // BLOCK,),
            in_specs=[
                pl.BlockSpec((BLOCK, depth, tile), lambda i, *_: (i, 0, 0)),
                pl.BlockSpec(source.shape, lambda i, *_: (0, 0, 0)),
            ],
            out_specs=pl.BlockSpec(out.shape, lambda i, *_: (0, 0, 0)),
            scratch_shapes=[pltpu.VMEM((blocks + 1, tile, width), jnp.float32)],
        ),
        compiler_params=pltpu.CompilerParams(vmem_limit_bytes=VMEM),
        cost_estimate=pl.CostEstimate(
            flops=slots * tile * tile * width * 2,
            bytes_accessed=bits.size * 4 + source.size * 4,
            transcendentals=0,
        ),
        name="backward_sweep",
    )(count, to_ids, from_ids, bits, source)


def pack_body(partial_ref, features_ref, out_ref):
    owners, rows, width = out_ref.shape
    nodes = partial_ref.shape[1]
    term = jnp.zeros((width, width), jnp.float32)
    for owner in range(owners):
        part = partial_ref[owner]
        out_ref[owner, :nodes] = part
        term += lax.dot_general(
            features_ref[owner], part, (((0,), (0,)), ((), ())), preferred_element_type=jnp.float32
        )
    for owner in range(owners):
        share = term[owner * (rows - nodes) : (owner + 1) * (rows - nodes)]
        out_ref[owner, nodes:] = share.astype(out_ref.dtype)


def pack(partial, features):
    owners, nodes, width = features.shape
    out = jax.ShapeDtypeStruct((owners, nodes + width // owners, width), jnp.bfloat16)
    whole = pl.BlockSpec(memory_space=pltpu.VMEM)
    return pl.pallas_call(
        pack_body,
        out_shape=out,
        in_specs=[whole, whole],
        out_specs=whole,
        cost_estimate=pl.CostEstimate(
            flops=features.size * width * 2, bytes_accessed=features.size * 6, transcendentals=0
        ),
        name="pack",
    )(partial, features)


def spread(block, axis):
    copies = lax.axis_size(axis)
    return lax.all_to_all(jnp.broadcast_to(block[None], (copies, *block.shape)), axis, 0, 0)


def swap_cores(block):
    return lax.ppermute(block, "col", [(i, i ^ 1) for i in range(lax.axis_size("col"))])


def swap_chips(block):
    return lax.ppermute(block, "col", [(i, i ^ 2) for i in range(lax.axis_size("col"))])


def from_below(block, distance):
    n_col = lax.axis_size("col")
    return lax.ppermute(block, "col", [(i, (i + 2 * distance) % n_col) for i in range(n_col)])


def per_device(features, cotangent, degrees, weight, tile_rows, tile_cols, tile_bits, tile_count):
    row_ids, col_ids, count = tile_rows[0, 0], tile_cols[0, 0], tile_count[0]
    tile = tile_bits.shape[-1]
    nodes, width = features.shape
    n_row, n_col = lax.axis_size("row"), lax.axis_size("col")
    n_z = n_col // 2
    place = lax.axis_index("col")
    core, z = place % 2, place // 2
    core_id = core.astype(jnp.int32)[None]
    degree = degrees[:, None].astype(jnp.float32)

    bits = tile_bits[0, 0]
    blocks = n_row * nodes // tile

    copies = jnp.broadcast_to(features[None], (n_row, nodes, width))
    source = lax.all_to_all(copies, "row", 0, 0)
    scaled = (cotangent.astype(jnp.float32) / degree).astype(jnp.bfloat16)
    own = jnp.stack([scaled] + [from_below(scaled, d) for d in range(1, n_z)])
    gradient = jnp.concatenate([own, swap_cores(own)])

    live = jnp.arange(row_ids.shape[0], dtype=jnp.int32) < count
    owner, half = row_ids // 2, row_ids % 2
    side = (owner % 2 != core) * n_z
    row_sources = (side + jnp.remainder(z - owner // 2, n_z)) * 2 + half
    apart = (owner // 2 + z) % 2 * (n_z // 2)
    away = jnp.remainder(owner // 4 - z // 2, n_z // 2)
    row_targets = (side + apart + away) * 2 + half
    row_targets = jnp.where(live, row_targets, blocks)
    col_targets = jnp.where(live, col_ids, blocks)

    partial = backward_sweep(
        count, col_targets, row_sources, bits, gradient.reshape(-1, tile, width)
    )
    partial = pack(partial.reshape(n_row, nodes, width), source)

    late, partial = lax.optimization_barrier((source, partial))
    shares = lax.all_to_all(partial, "row", 0, 0)
    kept, sent = forward_sweep(count, row_targets, col_ids, bits, late.reshape(-1, tile, width))
    chip = kept.astype(jnp.float32) + swap_cores(sent).astype(jnp.float32)
    chip = chip.reshape(2, n_z // 2, nodes, width)
    got = swap_chips(chip[1].astype(jnp.bfloat16))
    pair = (chip[0] + got.astype(jnp.float32)).astype(jnp.bfloat16)
    pieces = [pair[0]] + [from_below(pair[k], 2 * k) for k in range(1, n_z // 2)]
    summed = sum(p.astype(jnp.float32) for p in pieces)

    shares = shares.astype(jnp.float32).sum(0)
    term = spread(shares[nodes:], "col").sum(0)
    weight_grad = spread(term, "row").reshape(width, width)
    propagated = shares[:nodes].astype(jnp.bfloat16)
    input_grad = jnp.dot(propagated, weight.T, preferred_element_type=jnp.float32).astype(
        jnp.bfloat16
    )
    aggregated = (summed / degree).astype(jnp.bfloat16)
    output = jnp.dot(aggregated, weight, preferred_element_type=jnp.float32).astype(jnp.bfloat16)
    return output, weight_grad, input_grad


def solution(mesh):
    placed = (
        P(("col", "row"), None),
        P(("row", "col"), None),
        P(("row", "col")),
        P(),
        P("row", "col", None),
        P("row", "col", None),
        P("row", "col", None, None, None),
        P("row", "col"),
    )
    return jax.shard_map(
        per_device,
        mesh=mesh,
        in_specs=placed,
        out_specs=(P(("row", "col"), None), P(), P(("col", "row"), None)),
        check_vma=False,
    )
```
